256 devices in a mesh: row: 16 (over z, core), col: 16 (over x, y).
Axes of the slice: x: 4, y: 4, z: 8, core: 2. Of those that a mesh axis runs over, the one named last changes fastest.
Arguments:
- term_images: float32 [8, 4096, 4096], P(None, 'row', 'col'), may hold values from -6 to 6
- blur_width: float32 [8], replicated, may hold values from 0.8 to 6
- blur_coef: float32 [8], replicated, may hold values from -4 to 4
- direct_coef: float32 [8], replicated, may hold values from -1 to 1
- long_weight: float32 [8], replicated, may hold values from 0.2 to 2
- long_gain: float32 [1], replicated, may hold values from 0.5 to 1.5
- long_width: float32 [1], replicated, may hold values from 0.25 to 0.6
Outputs:
- resist_signal: float32 [4096, 4096], P('row', 'col')
The draws below stay inside these ranges and needn't reach their ends.
All inputs are finite; a program needn't handle non-finite values.
Results may differ from the reference program's by a relative error of at most 0.00002.
Values sent between devices are 32-bit elements; how exact they have to be, the bound alone decides.
No kernel may reach another device: no remote copies, remote signals or barrier semaphores. Data moves between devices by JAX's collectives and lax.ppermute only.
A program may use at most 64 MiB of HBM per device.

```python
import math
import jax
import jax.numpy as jnp
from jax import lax

K = 8
REACH = 16
LEVELS = 5
RC = 8
NH = 4096
NW = 4096


def levels(rng, extent, split, least, largest):
    gain, own = 1.0, jax.random.fold_in(rng, 6)
    for dim, blocks in split:
        heights = jnp.exp(jax.random.uniform(jax.random.fold_in(own, dim), (blocks,), jnp.float32, least / len(split), largest / len(split)))
        gain = gain * jnp.repeat(heights, extent[dim] // blocks).reshape([-1 if axis == dim else 1 for axis in range(len(extent))])
    return gain


def noise(key, dims, scale, most, pieces=(), held_as=jnp.bfloat16):
    array = jax.random.normal(key, dims, jnp.float32) * scale
    if len(pieces) > 0:
        array = levels(key, dims, pieces, -0.22, 0.18) * array
    return jnp.clip(array, min=-most, max=most).astype(held_as)


def setup_inputs(seed: int = 0) -> dict:
    streams_of = jax.random.split(jax.random.key(seed), 8)
    term_images = noise(streams_of[0], (K, NH, NW), 1.0, 6.0, ((1, 16), (2, 16)), jnp.float32)
    blur_width = jnp.clip(jnp.exp(jax.random.uniform(streams_of[1], (K,), jnp.float32, math.log(0.8), math.log(6.0))), 0.8, 6.0)
    blur_coef = jnp.clip(jax.random.uniform(streams_of[2], (K,), jnp.float32, -4.0, 4.0), -4.0, 4.0)
    direct_coef = jnp.clip(jax.random.uniform(streams_of[3], (K,), jnp.float32, -1.0, 1.0), -1.0, 1.0)
    long_weight = jnp.clip(jnp.exp(jax.random.uniform(streams_of[4], (K,), jnp.float32, math.log(0.2), math.log(2.0))), 0.2, 2.0)
    long_gain = jnp.clip(jax.random.uniform(streams_of[5], (1,), jnp.float32, 0.5, 1.5), 0.5, 1.5)
    long_width = jnp.clip(jnp.exp(jax.random.uniform(streams_of[6], (1,), jnp.float32, math.log(0.25), math.log(0.6))), 0.25, 0.6)
    return {"term_images": term_images, "blur_width": blur_width, "blur_coef": blur_coef, "direct_coef": direct_coef, "long_weight": long_weight, "long_gain": long_gain, "long_width": long_width}


BINOMIAL = (0.0625, 0.25, 0.375, 0.25, 0.0625)


def gauss_kernel(width, reach):
    offsets = jnp.arange(-reach, reach + 1).astype(jnp.float32)
    values = jnp.exp(-offsets * offsets / (2.0 * width[..., None] * width[..., None]))
    return values / jnp.sum(values, axis=-1, keepdims=True)


def zero_pad(values, margin):
    return jnp.pad(values, margin)


def coarsen(values, padder):
    row_count, col_count = values.shape
    padded = padder(values, 2)
    across = BINOMIAL[0] * padded[0:row_count, :]
    for tap_index in range(1, 5):
        across = across + BINOMIAL[tap_index] * padded[tap_index:tap_index + row_count, :]
    total = BINOMIAL[0] * across[:, 0:col_count]
    for tap_index in range(1, 5):
        total = total + BINOMIAL[tap_index] * across[:, tap_index:tap_index + col_count]
    return total[::2, ::2]


def refine(values, padder):
    row_count, col_count = values.shape
    padded = padder(values, 1)
    even_part = (padded[:-2] + 6.0 * padded[1:-1] + padded[2:]) * 0.125
    odd_part = (padded[1:-1] + padded[2:]) * 0.5
    rows_done = jnp.stack([even_part, odd_part], 1).reshape(2 * row_count, col_count + 2)
    even_part = (rows_done[:, :-2] + 6.0 * rows_done[:, 1:-1] + rows_done[:, 2:]) * 0.125
    odd_part = (rows_done[:, 1:-1] + rows_done[:, 2:]) * 0.5
    return jnp.stack([even_part, odd_part], 2).reshape(2 * row_count, 2 * col_count)


def coarse_blur(values, kernel, padder):
    row_count, col_count = values.shape
    padded = padder(values, RC)
    across = kernel[0] * padded[0:row_count, :]
    for tap_index in range(1, 2 * RC + 1):
        across = across + kernel[tap_index] * padded[tap_index:tap_index + row_count, :]
    total = kernel[0] * across[:, 0:col_count]
    for tap_index in range(1, 2 * RC + 1):
        total = total + kernel[tap_index] * across[:, tap_index:tap_index + col_count]
    return total


def reference(term_images, blur_width, blur_coef, direct_coef, long_weight, long_gain, long_width):
    kernels = gauss_kernel(blur_width, REACH)

    def advance(carry, inputs):
        local, source = carry
        image, kernel, coef_blur, coef_direct, weight = inputs
        padded = jnp.pad(image, ((0, 0), (REACH, REACH)))
        across = kernel[0] * padded[:, 0:NW]
        for tap_index in range(1, 2 * REACH + 1):
            across = across + kernel[tap_index] * padded[:, tap_index:tap_index + NW]
        padded = jnp.pad(across, ((REACH, REACH), (0, 0)))
        blurred = kernel[0] * padded[0:NH, :]
        for tap_index in range(1, 2 * REACH + 1):
            blurred = blurred + kernel[tap_index] * padded[tap_index:tap_index + NH, :]
        local = local + (coef_blur * blurred + coef_direct * image)
        source = source + weight * image * image
        return (local, source), None

    start = (jnp.zeros((NH, NW), jnp.float32), jnp.zeros((NH, NW), jnp.float32))
    (local, source), unused = lax.scan(advance, start, (term_images, kernels, blur_coef, direct_coef, long_weight))
    level_now = source
    for level_index in range(LEVELS):
        level_now = coarsen(level_now, zero_pad)
    coarse_kernel = gauss_kernel(long_width * RC, RC)[0]
    level_now = coarse_blur(level_now, coarse_kernel, zero_pad)
    for level_index in range(LEVELS):
        level_now = refine(level_now, zero_pad)
    return local + long_gain[0] * level_now
```

```python
import functools
import jax
import jax.numpy as jnp
import numpy as np
from jax import lax
from jax.experimental import pallas as pl
from jax.experimental.pallas import tpu as pltpu
from jax.sharding import PartitionSpec as P

K = 8
REACH = 16
LEVELS = 5
RC = 8
TILE = 256
EXT = TILE + 2 * REACH
CELLS = TILE >> LEVELS
SPAN = CELLS + 3
COUNT = 16
F32 = jnp.float32
BF16 = jnp.bfloat16


def pyramid_matrices():
    size = 4 * TILE
    down = np.eye(size)
    for _ in range(LEVELS):
        count = down.shape[0] // 2
        step = np.zeros((count, 2 * count))
        for i in range(count):
            for t, value in enumerate((1, 4, 6, 4, 1)):
                if 0 <= 2 * i + t - 2 < 2 * count:
                    step[i, 2 * i + t - 2] = value / 16
        down = step @ down
    up = np.eye(size >> LEVELS)
    for _ in range(LEVELS):
        count = up.shape[0]
        step = np.zeros((2 * count, count))
        for i in range(count):
            for j, value in ((i - 1, 1 / 8), (i, 6 / 8), (i + 1, 1 / 8)):
                if 0 <= j < count:
                    step[2 * i, j] = value
            for j in (i, i + 1):
                if j < count:
                    step[2 * i + 1, j] = 1 / 2
        up = step @ up
    down_tiles, up_tiles = np.zeros((3, 16, TILE)), np.zeros((3, 16, TILE))
    for n, tile in enumerate((0, 1, 3)):
        pixels = slice(tile * TILE, (tile + 1) * TILE)
        used = 0.0
        for i in range(SPAN):
            line = tile * CELLS - 1 + i
            if 0 <= line < size >> LEVELS:
                down_tiles[n, i] = down[line, pixels]
                up_tiles[n, i] = up[pixels, line]
        assert np.isclose(down_tiles[n].sum(), down[:, pixels].sum())
        assert np.isclose(up_tiles[n].sum(), up[pixels].sum())
    return down_tiles.astype(np.float32), up_tiles.astype(np.float32)


DOWN, UP = pyramid_matrices()


def swap_pairs(step, phase):
    partner = {}
    for i in range(COUNT):
        if (i // step) % 2 == phase:
            j = (i + step) % COUNT
            partner[i], partner[j] = j, i
    return sorted(partner.items())


def deltas(at):
    one = jnp.where(at % 2 == 0, 1, -1)
    two = jnp.where((at // 2) % 2 == 0, 2, -2)
    return (0, one, -one, two, -two)


def split(values):
    high = values.astype(BF16)
    return high, (values - high.astype(F32)).astype(BF16)


def dot(a, b, transposed=False):
    dims = (((1,), (1 if transposed else 0,)), ((), ()))
    return lax.dot_general(a, b, dims, preferred_element_type=F32)


def dot3(a, b, transposed=False):
    (ah, al), (bh, bl) = split(a), split(b)
    return dot(ah, bh, transposed) + (dot(ah, bl, transposed) + dot(al, bh, transposed))


def variant(at):
    return jnp.where(at == 0, 0, jnp.where(at == COUNT - 1, 2, 1))


def gauss(offsets, width, reach):
    wide = jnp.full((1, 128), width, F32)
    scale = -0.5 / (wide * wide)
    taps = (lax.broadcasted_iota(jnp.int32, (1, 128), 1) - reach).astype(F32)
    total = jnp.sum(
        jnp.where(jnp.abs(taps) <= reach, jnp.exp(taps * taps * scale), 0.0), axis=1, keepdims=True
    )
    far = offsets.astype(F32)
    values = jnp.exp(far * far * scale) * (1.0 / total)
    return jnp.where(jnp.abs(far) <= reach, values, 0.0)


def coarse_band(at, width):
    line = lax.broadcasted_iota(jnp.int32, (16, 128), 0)
    lane = lax.broadcasted_iota(jnp.int32, (16, 128), 1)
    block, cell = lane // 16, lane % 16
    delta = jnp.zeros((16, 128), jnp.int32)
    for n, value in enumerate(deltas(at)):
        delta = jnp.where(block == n, value, delta)
    inside = (at + delta >= 0) & (at + delta < COUNT) & (block < 5) & (cell < SPAN) & (line < SPAN)
    return jnp.where(inside, gauss(8 * delta + cell - line, width * RC, RC), 0.0)


def first_kernel(
    width, blur, direct, weight, down, images,
    even_out, odd_out, far_out, local_out, side_out,
    held, kh, kl, yh, yl, eh, el, sems,
):
    row, col = lax.axis_index("row"), lax.axis_index("col")
    copies = [pltpu.make_async_copy(images.at[k], held.at[k], sems.at[k]) for k in range(K)]
    for copy in copies:
        copy.start()
    offsets = (
        lax.broadcasted_iota(jnp.int32, (TILE // 2 + 32, 128), 1)
        - lax.broadcasted_iota(jnp.int32, (TILE // 2 + 32, 128), 0)
        + REACH
    )
    half = TILE // 2
    none = jnp.zeros((half, 128), BF16)
    for k in range(K):
        for full, edge, band in zip((kh, kl), (eh, el), split(gauss(offsets, width[k], REACH))):
            full[k, 0 : half + 32, 0:half] = band
            full[k, half + 32 : EXT, 0:half] = none
            full[k, 0:half, half:TILE] = none
            full[k, half:EXT, half:TILE] = band
            edge[0:16, TILE * k : TILE * k + half] = band[0:16]
            edge[0:16, TILE * k + half : TILE * (k + 1)] = none[0:16]
            edge[16:32, TILE * k : TILE * k + half] = none[0:16]
            edge[16:32, TILE * k + half : TILE * (k + 1)] = band[half + 16 : half + 32]
    source = jnp.zeros((TILE, TILE), F32)
    plain = jnp.zeros((TILE, TILE), F32)
    for k in range(K):
        copies[k].wait()
        image = held[k]
        source = source + weight[k] * image * image
        plain = plain + direct[k] * image
        xh, xl = split(image)
        tall = dot(kh[k], xh) + (dot(kh[k], xl) + dot(kl[k], xh))
        high, low = split(tall * blur[k])
        yh[:, TILE * k : TILE * (k + 1)] = high
        yl[:, TILE * k : TILE * (k + 1)] = low
    th = kh[:, 16 : 16 + TILE, :].reshape(K * TILE, TILE)
    tl = kl[:, 16 : 16 + TILE, :].reshape(K * TILE, TILE)
    wide = dot(yh[...], th) + (dot(yl[...], th) + dot(yh[...], tl))
    side = dot(eh[...], yh[...], True) + (dot(eh[...], yl[...], True) + dot(el[...], yh[...], True))
    local_out[...] = wide[16 : 16 + TILE] + plain
    side_out[...] = side[:, 16 : 16 + TILE]
    cells = dot3(dot3(down[variant(row)], source), down[variant(col)], True)
    lane = lax.broadcasted_iota(jnp.int32, (16, 128), 1)
    far = jnp.concatenate([cells, jnp.zeros((16, 112), F32)], axis=1)
    far_out[...] = far

    def message(at):
        corners = [side[0:16, at : at + 16], side[16:32, at : at + 16]]
        tail = jnp.concatenate([cells, *corners, jnp.zeros((16, 80), F32)], axis=1)
        return wide[at : at + 16], tail

    def put(out, parts):
        out[:, 0:TILE] = parts[0]
        out[:, TILE : TILE + 128] = parts[1]

    top, bottom = message(0), message(EXT - 16)

    @pl.when(row % 2 == 0)
    def _():
        put(even_out, bottom)
        put(odd_out, top)

    @pl.when(row % 2 == 1)
    def _():
        put(even_out, top)
        put(odd_out, bottom)


def stacked(parts):
    return jnp.concatenate([*parts, jnp.zeros((128 - 16 * len(parts), 128), F32)], axis=0)


def middle_kernel(wide, even, odd, far_a, far_b, own, side, even_out, odd_out, far_out):
    row, col = lax.axis_index("row"), lax.axis_index("col")
    parts = stacked([own[...], even[:, TILE:], odd[:, TILE:], far_a[...], far_b[...]])
    cells = dot3(coarse_band(row, wide[0]), parts)
    lane = lax.broadcasted_iota(jnp.int32, (16, 128), 1)
    cells = jnp.where(lane < 16, cells, 0.0)
    turned = jnp.transpose(stacked([cells]))[0:16]
    far_out[...] = turned
    is_even = row % 2 == 0
    tail_e, tail_o = even[:, TILE:], odd[:, TILE:]
    above = jnp.where(row > 0, jnp.where(is_even, tail_o, tail_e), 0.0)
    below = jnp.where(row < COUNT - 1, jnp.where(is_even, tail_e, tail_o), 0.0)
    blank = jnp.zeros((16, TILE - 32), F32)

    def strip(n):
        at = 16 * (n + 1)
        more = jnp.concatenate([above[:, at : at + 16], blank, below[:, at : at + 16]], axis=1)
        return side[16 * n : 16 * n + 16] + more

    left, right = strip(0), strip(1)
    even_out[:, TILE:] = turned
    odd_out[:, TILE:] = turned

    @pl.when(col % 2 == 0)
    def _():
        even_out[:, 0:TILE] = right
        odd_out[:, 0:TILE] = left

    @pl.when(col % 2 == 1)
    def _():
        even_out[:, 0:TILE] = left
        odd_out[:, 0:TILE] = right


def last_kernel(wide, gain, up, local, row_e, row_o, col_e, col_o, far_a, far_b, own, out):
    row, col = lax.axis_index("row"), lax.axis_index("col")
    parts = stacked([own[...], col_e[:, TILE:], col_o[:, TILE:], far_a[...], far_b[...]])
    cells = dot3(coarse_band(col, wide[0]), parts)
    pad = jnp.zeros((112, TILE), F32)
    lines = dot3(cells, jnp.concatenate([up[variant(row)], pad], axis=0)) * gain[0]
    is_even = col % 2 == 0
    strip_e, strip_o = col_e[:, 0:TILE], col_o[:, 0:TILE]
    left = jnp.where(col > 0, jnp.where(is_even, strip_o, strip_e), 0.0)
    right = jnp.where(col < COUNT - 1, jnp.where(is_even, strip_e, strip_o), 0.0)
    turned = jnp.transpose(
        jnp.concatenate([left, pad[0:16], lines, pad[0:64], right], axis=0)
    )
    spread = jnp.concatenate([pad[0:32], up[variant(col)], pad[0:80]], axis=0)
    lane = lax.broadcasted_iota(jnp.int32, (TILE, 128), 1)
    whole = local[...] + dot3(jnp.where((lane >= 32) & (lane < 48), turned, 0.0), spread)
    out[:, 0:128] = whole[:, 0:128] + jnp.where(lane < 16, turned, 0.0)
    out[:, 128:TILE] = whole[:, 128:TILE] + jnp.where(lane >= 112, turned, 0.0)
    is_even = row % 2 == 0
    strip_e, strip_o = row_e[:, 0:TILE], row_o[:, 0:TILE]
    out[0:16, :] += jnp.where(row > 0, jnp.where(is_even, strip_o, strip_e), 0.0)
    out[TILE - 16 : TILE, :] += jnp.where(
        row < COUNT - 1, jnp.where(is_even, strip_e, strip_o), 0.0
    )


SCALAR = pl.BlockSpec(memory_space=pltpu.SMEM)
VECTOR = pl.BlockSpec(memory_space=pltpu.VMEM)


def shapes(*dims):
    return [jax.ShapeDtypeStruct(d, F32) for d in dims]


def swap(values, axis, step, phase):
    return lax.ppermute(values, axis, swap_pairs(step, phase))


def on_device(term_images, blur_width, blur_coef, direct_coef, long_weight, long_gain, long_width):
    message, tiny = (16, TILE + 128), (16, 128)
    even, odd, far, local, side = pl.pallas_call(
        first_kernel,
        out_shape=shapes(message, message, tiny, (TILE, TILE), (32, TILE)),
        in_specs=[SCALAR] * 4 + [VECTOR, pl.BlockSpec(memory_space=pl.ANY)],
        out_specs=[VECTOR] * 5,
        scratch_shapes=[
            pltpu.VMEM((K, TILE, TILE), F32),
            pltpu.VMEM((K, EXT, TILE), BF16),
            pltpu.VMEM((K, EXT, TILE), BF16),
            pltpu.VMEM((EXT, K * TILE), BF16),
            pltpu.VMEM((EXT, K * TILE), BF16),
            pltpu.VMEM((32, K * TILE), BF16),
            pltpu.VMEM((32, K * TILE), BF16),
            pltpu.SemaphoreType.DMA((K,)),
        ],
        name="blur_tile",
    )(blur_width, blur_coef, direct_coef, long_weight, jnp.asarray(DOWN), term_images)
    row_e, row_o = swap(even, "row", 1, 0), swap(odd, "row", 1, 1)
    row_a, row_b = swap(far, "row", 2, 0), swap(far, "row", 2, 1)
    even, odd, turned = pl.pallas_call(
        middle_kernel,
        out_shape=shapes(message, message, tiny),
        in_specs=[SCALAR] + [VECTOR] * 6,
        out_specs=[VECTOR] * 3,
        name="join_rows",
    )(long_width, row_e, row_o, row_a, row_b, far, side)
    col_e, col_o = swap(even, "col", 1, 0), swap(odd, "col", 1, 1)
    col_a, col_b = swap(turned, "col", 2, 0), swap(turned, "col", 2, 1)
    return pl.pallas_call(
        last_kernel,
        out_shape=jax.ShapeDtypeStruct((TILE, TILE), F32),
        in_specs=[SCALAR] * 2 + [VECTOR] * 9,
        out_specs=VECTOR,
        name="join_columns",
    )(long_width, long_gain, jnp.asarray(UP), local, row_e, row_o, col_e, col_o, col_a, col_b, turned)


def solution(mesh):
    placed = (P(None, "row", "col"), P(), P(), P(), P(), P(), P())
    return jax.shard_map(
        on_device, mesh=mesh, in_specs=placed, out_specs=P("row", "col"), check_vma=False
    )
```

```python
import functools
import jax
import jax.numpy as jnp
import numpy as np
from jax import lax
from jax.experimental import pallas as pl
from jax.experimental.pallas import tpu as pltpu
from jax.sharding import PartitionSpec as P

K = 8
REACH = 16
LEVELS = 5
RC = 8
TILE = 256
EXT = TILE + 2 * REACH
CELLS = TILE >> LEVELS
SPAN = CELLS + 3
COUNT = 16
F32 = jnp.float32
BF16 = jnp.bfloat16


def pyramid_matrices():
    size = 4 * TILE
    down = np.eye(size)
    for _ in range(LEVELS):
        count = down.shape[0] // 2
        step = np.zeros((count, 2 * count))
        for i in range(count):
            for t, value in enumerate((1, 4, 6, 4, 1)):
                if 0 <= 2 * i + t - 2 < 2 * count:
                    step[i, 2 * i + t - 2] = value / 16
        down = step @ down
    up = np.eye(size >> LEVELS)
    for _ in range(LEVELS):
        count = up.shape[0]
        step = np.zeros((2 * count, count))
        for i in range(count):
            for j, value in ((i - 1, 1 / 8), (i, 6 / 8), (i + 1, 1 / 8)):
                if 0 <= j < count:
                    step[2 * i, j] = value
            for j in (i, i + 1):
                if j < count:
                    step[2 * i + 1, j] = 1 / 2
        up = step @ up
    down_tiles, up_tiles = np.zeros((3, 16, TILE)), np.zeros((3, 16, TILE))
    for n, tile in enumerate((0, 1, 3)):
        pixels = slice(tile * TILE, (tile + 1) * TILE)
        used = 0.0
        for i in range(SPAN):
            line = tile * CELLS - 1 + i
            if 0 <= line < size >> LEVELS:
                down_tiles[n, i] = down[line, pixels]
                up_tiles[n, i] = up[pixels, line]
        assert np.isclose(down_tiles[n].sum(), down[:, pixels].sum())
        assert np.isclose(up_tiles[n].sum(), up[pixels].sum())
    return down_tiles.astype(np.float32), up_tiles.astype(np.float32)


DOWN, UP = pyramid_matrices()


def swap_pairs(axis, step, phase):
    partner = {}
    for i in range(COUNT - step):
        if (i // step) % 2 == phase:
            partner[i], partner[i + step] = i + step, i
    pairs = []
    for r in range(COUNT):
        for c in range(COUNT):
            if (r if axis == "row" else c) in partner:
                other = (partner[r], c) if axis == "row" else (r, partner[c])
            else:
                other = (r, c ^ 1) if axis == "row" and step == 1 else (r ^ 1, c)
            pairs.append((r * COUNT + c, other[0] * COUNT + other[1]))
    return pairs


def deltas(at):
    one = jnp.where(at % 2 == 0, 1, -1)
    two = jnp.where((at // 2) % 2 == 0, 2, -2)
    return (0, one, -one, two, -two)


def split(values):
    high = values.astype(BF16)
    return high, (values - high.astype(F32)).astype(BF16)


def dot(a, b, transposed=False):
    dims = (((1,), (1 if transposed else 0,)), ((), ()))
    return lax.dot_general(a, b, dims, preferred_element_type=F32)


def dot3(a, b, transposed=False):
    (ah, al), (bh, bl) = split(a), split(b)
    return dot(ah, bh, transposed) + (dot(ah, bl, transposed) + dot(al, bh, transposed))


def variant(at):
    return jnp.where(at == 0, 0, jnp.where(at == COUNT - 1, 2, 1))


def gauss(offsets, width, reach):
    wide = jnp.full((1, 128), width, F32)
    scale = -0.5 / (wide * wide)
    taps = (lax.broadcasted_iota(jnp.int32, (1, 128), 1) - reach).astype(F32)
    total = jnp.sum(
        jnp.where(jnp.abs(taps) <= reach, jnp.exp(taps * taps * scale), 0.0), axis=1, keepdims=True
    )
    far = offsets.astype(F32)
    values = jnp.exp(far * far * scale) * (1.0 / total)
    return jnp.where(jnp.abs(far) <= reach, values, 0.0)


def coarse_band(at, width):
    line = lax.broadcasted_iota(jnp.int32, (16, 128), 0)
    lane = lax.broadcasted_iota(jnp.int32, (16, 128), 1)
    block, cell = lane // 16, lane % 16
    delta = jnp.zeros((16, 128), jnp.int32)
    for n, value in enumerate(deltas(at)):
        delta = jnp.where(block == n, value, delta)
    inside = (at + delta >= 0) & (at + delta < COUNT) & (block < 5) & (cell < SPAN) & (line < SPAN)
    return jnp.where(inside, gauss(8 * delta + cell - line, width * RC, RC), 0.0)


def first_kernel(
    width_in, blur_in, direct_in, weight_in, down_in, images,
    even_out, odd_out, far_out, local_out, side_out,
    held, kh, kl, yh, yl, eh, el, width, blur, direct, weight, down, sems,
):
    row, col = lax.axis_index("row"), lax.axis_index("col")
    small = [
        pltpu.make_async_copy(source, target, sems.at[K + n])
        for n, (source, target) in enumerate(
            (
                (width_in, width),
                (blur_in, blur),
                (direct_in, direct),
                (weight_in, weight),
                (down_in.at[variant(row)], down.at[0]),
                (down_in.at[variant(col)], down.at[1]),
            )
        )
    ]
    copies = [pltpu.make_async_copy(images.at[k], held.at[k], sems.at[k]) for k in range(K)]
    for copy in small + copies:
        copy.start()
    for copy in small:
        copy.wait()
    offsets = (
        lax.broadcasted_iota(jnp.int32, (TILE // 2 + 32, 128), 1)
        - lax.broadcasted_iota(jnp.int32, (TILE // 2 + 32, 128), 0)
        + REACH
    )
    half = TILE // 2
    none = jnp.zeros((half, 128), BF16)
    for k in range(K):
        for full, edge, band in zip((kh, kl), (eh, el), split(gauss(offsets, width[k], REACH))):
            full[k, 0 : half + 32, 0:half] = band
            full[k, half + 32 : EXT, 0:half] = none
            full[k, 0:half, half:TILE] = none
            full[k, half:EXT, half:TILE] = band
            edge[0:16, TILE * k : TILE * k + half] = band[0:16]
            edge[0:16, TILE * k + half : TILE * (k + 1)] = none[0:16]
            edge[16:32, TILE * k : TILE * k + half] = none[0:16]
            edge[16:32, TILE * k + half : TILE * (k + 1)] = band[half + 16 : half + 32]
    source = jnp.zeros((TILE, TILE), F32)
    plain = jnp.zeros((TILE, TILE), F32)
    for k in range(K):
        copies[k].wait()
        image = held[k]
        source = source + weight[k] * image * image
        plain = plain + direct[k] * image
        xh, xl = split(image)
        tall = dot(kh[k], xh) + (dot(kh[k], xl) + dot(kl[k], xh))
        high, low = split(tall * blur[k])
        yh[:, TILE * k : TILE * (k + 1)] = high
        yl[:, TILE * k : TILE * (k + 1)] = low
    th = kh[:, 16 : 16 + TILE, :].reshape(K * TILE, TILE)
    tl = kl[:, 16 : 16 + TILE, :].reshape(K * TILE, TILE)
    wide = dot(yh[...], th) + (dot(yl[...], th) + dot(yh[...], tl))
    side = dot(eh[...], yh[...], True) + (dot(eh[...], yl[...], True) + dot(el[...], yh[...], True))
    local_out[...] = wide[16 : 16 + TILE] + plain
    side_out[...] = side[:, 16 : 16 + TILE]
    cells = dot3(dot3(down[0], source), down[1], True)
    lane = lax.broadcasted_iota(jnp.int32, (16, 128), 1)
    far = jnp.concatenate([cells, jnp.zeros((16, 112), F32)], axis=1)
    far_out[...] = far

    def message(at):
        corners = [side[0:16, at : at + 16], side[16:32, at : at + 16]]
        tail = jnp.concatenate([cells, *corners, jnp.zeros((16, 80), F32)], axis=1)
        return wide[at : at + 16], tail

    def put(out, parts):
        out[:, 0:TILE] = parts[0]
        out[:, TILE : TILE + 128] = parts[1]

    top, bottom = message(0), message(EXT - 16)

    @pl.when(row % 2 == 0)
    def _():
        put(even_out, bottom)
        put(odd_out, top)

    @pl.when(row % 2 == 1)
    def _():
        put(even_out, top)
        put(odd_out, bottom)


def stacked(parts):
    return jnp.concatenate([*parts, jnp.zeros((128 - 16 * len(parts), 128), F32)], axis=0)


def middle_kernel(wide, even, odd, far_a, far_b, own, side, even_out, odd_out, far_out):
    row, col = lax.axis_index("row"), lax.axis_index("col")
    parts = stacked([own[...], even[:, TILE:], odd[:, TILE:], far_a[...], far_b[...]])
    cells = dot3(coarse_band(row, wide[0]), parts)
    lane = lax.broadcasted_iota(jnp.int32, (16, 128), 1)
    cells = jnp.where(lane < 16, cells, 0.0)
    turned = jnp.transpose(stacked([cells]))[0:16]
    far_out[...] = turned
    is_even = row % 2 == 0
    tail_e, tail_o = even[:, TILE:], odd[:, TILE:]
    above = jnp.where(row > 0, jnp.where(is_even, tail_o, tail_e), 0.0)
    below = jnp.where(row < COUNT - 1, jnp.where(is_even, tail_e, tail_o), 0.0)
    blank = jnp.zeros((16, TILE - 32), F32)

    def strip(n):
        at = 16 * (n + 1)
        more = jnp.concatenate([above[:, at : at + 16], blank, below[:, at : at + 16]], axis=1)
        return side[16 * n : 16 * n + 16] + more

    left, right = strip(0), strip(1)
    even_out[:, TILE:] = turned
    odd_out[:, TILE:] = turned

    @pl.when(col % 2 == 0)
    def _():
        even_out[:, 0:TILE] = right
        odd_out[:, 0:TILE] = left

    @pl.when(col % 2 == 1)
    def _():
        even_out[:, 0:TILE] = left
        odd_out[:, 0:TILE] = right


def last_kernel(wide, gain, up, local, row_e, row_o, col_e, col_o, far_a, far_b, own, out):
    row, col = lax.axis_index("row"), lax.axis_index("col")
    parts = stacked([own[...], col_e[:, TILE:], col_o[:, TILE:], far_a[...], far_b[...]])
    cells = dot3(coarse_band(col, wide[0]), parts)
    pad = jnp.zeros((112, TILE), F32)
    lines = dot3(cells, jnp.concatenate([up[variant(row)], pad], axis=0)) * gain[0]
    is_even = col % 2 == 0
    strip_e, strip_o = col_e[:, 0:TILE], col_o[:, 0:TILE]
    left = jnp.where(col > 0, jnp.where(is_even, strip_o, strip_e), 0.0)
    right = jnp.where(col < COUNT - 1, jnp.where(is_even, strip_e, strip_o), 0.0)
    turned = jnp.transpose(
        jnp.concatenate([left, pad[0:16], lines, pad[0:64], right], axis=0)
    )
    spread = jnp.concatenate([pad[0:32], up[variant(col)], pad[0:80]], axis=0)
    lane = lax.broadcasted_iota(jnp.int32, (TILE, 128), 1)
    whole = local[...] + dot3(jnp.where((lane >= 32) & (lane < 48), turned, 0.0), spread)
    out[:, 0:128] = whole[:, 0:128] + jnp.where(lane < 16, turned, 0.0)
    out[:, 128:TILE] = whole[:, 128:TILE] + jnp.where(lane >= 112, turned, 0.0)
    is_even = row % 2 == 0
    strip_e, strip_o = row_e[:, 0:TILE], row_o[:, 0:TILE]
    out[0:16, :] += jnp.where(row > 0, jnp.where(is_even, strip_o, strip_e), 0.0)
    out[TILE - 16 : TILE, :] += jnp.where(
        row < COUNT - 1, jnp.where(is_even, strip_e, strip_o), 0.0
    )


SCALAR = pl.BlockSpec(memory_space=pltpu.SMEM)
VECTOR = pl.BlockSpec(memory_space=pltpu.VMEM)


def shapes(*dims):
    return [jax.ShapeDtypeStruct(d, F32) for d in dims]


def swap(values, axis, step, phase):
    return lax.ppermute(values, ("row", "col"), swap_pairs(axis, step, phase))


def on_device(term_images, blur_width, blur_coef, direct_coef, long_weight, long_gain, long_width):
    message, tiny = (16, TILE + 128), (16, 128)
    even, odd, far, local, side = pl.pallas_call(
        first_kernel,
        out_shape=shapes(message, message, tiny, (TILE, TILE), (32, TILE)),
        in_specs=[pl.BlockSpec(memory_space=pltpu.HBM)] * 6,
        out_specs=[VECTOR] * 5,
        scratch_shapes=[
            pltpu.VMEM((K, TILE, TILE), F32),
            pltpu.VMEM((K, EXT, TILE), BF16),
            pltpu.VMEM((K, EXT, TILE), BF16),
            pltpu.VMEM((EXT, K * TILE), BF16),
            pltpu.VMEM((EXT, K * TILE), BF16),
            pltpu.VMEM((32, K * TILE), BF16),
            pltpu.VMEM((32, K * TILE), BF16),
            *[pltpu.SMEM((K,), F32)] * 4,
            pltpu.VMEM((2, 16, TILE), F32),
            pltpu.SemaphoreType.DMA((K + 6,)),
        ],
        compiler_params=pltpu.CompilerParams(vmem_limit_bytes=24 << 20),
        name="blur_tile",
    )(*[
        pltpu.with_memory_space_constraint(value, pltpu.HBM)
        for value in (blur_width, blur_coef, direct_coef, long_weight, jnp.asarray(DOWN), term_images)
    ])
    row_e, row_o = swap(even, "row", 1, 0), swap(odd, "row", 1, 1)
    row_a, row_b = swap(far, "row", 2, 0), swap(far, "row", 2, 1)
    even, odd, turned = pl.pallas_call(
        middle_kernel,
        out_shape=shapes(message, message, tiny),
        in_specs=[SCALAR] + [VECTOR] * 6,
        out_specs=[VECTOR] * 3,
        compiler_params=pltpu.CompilerParams(vmem_limit_bytes=4 << 20),
        name="join_rows",
    )(long_width, row_e, row_o, row_a, row_b, far, side)
    col_e, col_o = swap(even, "col", 1, 0), swap(odd, "col", 1, 1)
    col_a, col_b = swap(turned, "col", 2, 0), swap(turned, "col", 2, 1)
    return pl.pallas_call(
        last_kernel,
        out_shape=jax.ShapeDtypeStruct((TILE, TILE), F32),
        in_specs=[SCALAR] * 2 + [VECTOR] * 9,
        out_specs=VECTOR,
        compiler_params=pltpu.CompilerParams(vmem_limit_bytes=8 << 20),
        name="join_columns",
    )(long_width, long_gain, jnp.asarray(UP), local, row_e, row_o, col_e, col_o, col_a, col_b, turned)


def solution(mesh):
    placed = (P(None, "row", "col"), P(), P(), P(), P(), P(), P())
    return jax.shard_map(
        on_device, mesh=mesh, in_specs=placed, out_specs=P("row", "col"), check_vma=False
    )
```

```python
import functools
import jax
import jax.numpy as jnp
import numpy as np
from jax import lax
from jax.experimental import pallas as pl
from jax.experimental.pallas import tpu as pltpu
from jax.sharding import PartitionSpec as P

K = 8
REACH = 16
LEVELS = 5
RC = 8
TILE = 256
EXT = TILE + 2 * REACH
CELLS = TILE >> LEVELS
SPAN = CELLS + 3
COUNT = 16
F32 = jnp.float32
BF16 = jnp.bfloat16


def pyramid_matrices():
    size = 4 * TILE
    down = np.eye(size)
    for _ in range(LEVELS):
        count = down.shape[0] // 2
        step = np.zeros((count, 2 * count))
        for i in range(count):
            for t, value in enumerate((1, 4, 6, 4, 1)):
                if 0 <= 2 * i + t - 2 < 2 * count:
                    step[i, 2 * i + t - 2] = value / 16
        down = step @ down
    up = np.eye(size >> LEVELS)
    for _ in range(LEVELS):
        count = up.shape[0]
        step = np.zeros((2 * count, count))
        for i in range(count):
            for j, value in ((i - 1, 1 / 8), (i, 6 / 8), (i + 1, 1 / 8)):
                if 0 <= j < count:
                    step[2 * i, j] = value
            for j in (i, i + 1):
                if j < count:
                    step[2 * i + 1, j] = 1 / 2
        up = step @ up
    down_tiles, up_tiles = np.zeros((3, 16, TILE)), np.zeros((3, 16, TILE))
    for n, tile in enumerate((0, 1, 3)):
        pixels = slice(tile * TILE, (tile + 1) * TILE)
        used = 0.0
        for i in range(SPAN):
            line = tile * CELLS - 1 + i
            if 0 <= line < size >> LEVELS:
                down_tiles[n, i] = down[line, pixels]
                up_tiles[n, i] = up[pixels, line]
        assert np.isclose(down_tiles[n].sum(), down[:, pixels].sum())
        assert np.isclose(up_tiles[n].sum(), up[pixels].sum())
    return down_tiles.astype(np.float32), up_tiles.astype(np.float32)


DOWN, UP = pyramid_matrices()


def swap_pairs(axis, step, phase):
    partner = {}
    for i in range(COUNT - step):
        if (i // step) % 2 == phase:
            partner[i], partner[i + step] = i + step, i
    pairs = []
    for r in range(COUNT):
        for c in range(COUNT):
            if (r if axis == "row" else c) in partner:
                other = (partner[r], c) if axis == "row" else (r, partner[c])
            else:
                other = (r, c ^ 1) if axis == "row" and step == 1 else (r ^ 1, c)
            pairs.append((r * COUNT + c, other[0] * COUNT + other[1]))
    return pairs


def deltas(at):
    one = jnp.where(at % 2 == 0, 1, -1)
    two = jnp.where((at // 2) % 2 == 0, 2, -2)
    return (0, one, -one, two, -two)


def split(values):
    high = values.astype(BF16)
    return high, (values - high.astype(F32)).astype(BF16)


def dot(a, b, transposed=False):
    dims = (((1,), (1 if transposed else 0,)), ((), ()))
    return lax.dot_general(a, b, dims, preferred_element_type=F32)


def dot3(a, b, transposed=False):
    (ah, al), (bh, bl) = split(a), split(b)
    return dot(ah, bh, transposed) + (dot(ah, bl, transposed) + dot(al, bh, transposed))


def variant(at):
    return jnp.where(at == 0, 0, jnp.where(at == COUNT - 1, 2, 1))


def gauss(offsets, width, reach):
    wide = jnp.full((1, 128), width, F32)
    scale = -0.5 / (wide * wide)
    taps = (lax.broadcasted_iota(jnp.int32, (1, 128), 1) - reach).astype(F32)
    total = jnp.sum(
        jnp.where(jnp.abs(taps) <= reach, jnp.exp(taps * taps * scale), 0.0), axis=1, keepdims=True
    )
    far = offsets.astype(F32)
    values = jnp.exp(far * far * scale) * (1.0 / total)
    return jnp.where(jnp.abs(far) <= reach, values, 0.0)


def coarse_band(at, width):
    line = lax.broadcasted_iota(jnp.int32, (16, 128), 0)
    lane = lax.broadcasted_iota(jnp.int32, (16, 128), 1)
    block, cell = lane // 16, lane % 16
    delta = jnp.zeros((16, 128), jnp.int32)
    for n, value in enumerate(deltas(at)):
        delta = jnp.where(block == n, value, delta)
    inside = (at + delta >= 0) & (at + delta < COUNT) & (block < 5) & (cell < SPAN) & (line < SPAN)
    return jnp.where(inside, gauss(8 * delta + cell - line, width * RC, RC), 0.0)


def edge_band(width):
    line = lax.broadcasted_iota(jnp.int32, (32, TILE), 0)
    lane = lax.broadcasted_iota(jnp.int32, (32, TILE), 1)
    image, place = lane // 32, lane % 32
    wide = jnp.full((32, TILE), width[0], F32)
    for k in range(1, K):
        wide = jnp.where(image == k, width[k], wide)
    scale = -0.5 / (wide * wide)
    far = jnp.where(line < 16, place + 16 - line, place - 16 - line)
    valid = (jnp.abs(far) <= REACH) & ((line < 16) == (place < 16))
    row_scale = scale[0:8]
    total = jnp.full((8, TILE), 0.5, F32)
    for t in range(1, REACH + 1):
        total = total + jnp.exp(float(t * t) * row_scale)
    share = 0.5 / total
    share = jnp.concatenate([share] * 4, axis=0)
    far = far.astype(F32)
    return jnp.where(valid, jnp.exp(far * far * scale) * share, 0.0)


def first_kernel(
    width_in, blur_in, weight_in, down_in, images,
    even_out, odd_out, far_out, side_out, th, tl, held,
    eh, el, zone, width, blur, weight, down, sems,
):
    row, col = lax.axis_index("row"), lax.axis_index("col")
    small = [
        pltpu.make_async_copy(source, target, sems.at[K + n])
        for n, (source, target) in enumerate(
            (
                (width_in, width),
                (blur_in, blur),
                (weight_in, weight),
                (down_in.at[variant(row)], down.at[0]),
                (down_in.at[variant(col)], down.at[1]),
            )
        )
    ]
    copies = [pltpu.make_async_copy(images.at[k], held.at[k], sems.at[k]) for k in range(K)]
    for copy in small + copies:
        copy.start()
    for copy in small:
        copy.wait()
    half = TILE // 2
    offsets = (
        lax.broadcasted_iota(jnp.int32, (half + 32, 128), 1)
        - lax.broadcasted_iota(jnp.int32, (half + 32, 128), 0)
        + REACH
    )
    none = jnp.zeros((half, 128), BF16)
    for k in range(K):
        for full, edge, band in zip((th, tl), (eh, el), split(gauss(offsets, width[k], REACH))):
            full[k, 0 : half + 16, 0:half] = band[16 : half + 32]
            full[k, half + 16 : TILE, 0:half] = none[16:]
            full[k, 0 : half - 16, half:TILE] = none[16:]
            full[k, half - 16 : TILE, half:TILE] = band[0 : half + 16]
            edge[0:16, TILE * k : TILE * k + half] = band[0:16]
            edge[0:16, TILE * k + half : TILE * (k + 1)] = none[0:16]
            edge[16:32, TILE * k : TILE * k + half] = none[0:16]
            edge[16:32, TILE * k + half : TILE * (k + 1)] = band[half + 16 : half + 32]
    ends = split(edge_band(width))
    zone[:, 2 * TILE :] = jnp.zeros((TILE, 128), F32)
    lane = lax.broadcasted_iota(jnp.int32, (TILE, 128), 1)
    source = jnp.zeros((TILE, TILE), F32)
    for copy in copies:
        copy.wait()
    for k in range(K):
        image = held[k]
        source = source + weight[k] * image * image
        turned = jnp.transpose(jnp.where(lane < 64, image[:, 0:128], image[:, 128:TILE]))
        lines = [image[0:16], image[TILE - 16 : TILE], turned[0:16], turned[112:128]]
        ah, al = split(jnp.concatenate(lines, axis=0) * blur[k])
        done = dot(ah, th[k]) + (dot(al, th[k]) + dot(ah, tl[k]))
        zone[32 * k : 32 * k + 32, 0:TILE] = done[0:32]
        zone[32 * k : 32 * k + 32, TILE : 2 * TILE] = done[32:64]
        part = slice(TILE * k, TILE * (k + 1))
        zone[32 * k : 32 * k + 32, 2 * TILE : 2 * TILE + 32] = dot(
            ah[32:64], eh[:, part], True
        ) + (dot(al[32:64], eh[:, part], True) + dot(ah[32:64], el[:, part], True))
    zh, zl = split(zone[...])
    strips = dot(ends[0], zh) + (dot(ends[1], zh) + dot(ends[0], zl))
    side_out[...] = strips[:, TILE : 2 * TILE]
    cells = dot3(dot3(down[0], source), down[1], True)
    far_out[...] = jnp.concatenate([cells, jnp.zeros((16, 112), F32)], axis=1)

    def message(n):
        at = 2 * TILE + 16 * n
        corners = [strips[0:16, at : at + 16], strips[16:32, at : at + 16]]
        tail = jnp.concatenate([cells, *corners, jnp.zeros((16, 80), F32)], axis=1)
        return strips[16 * n : 16 * n + 16, 0:TILE], tail

    def put(out, parts):
        out[:, 0:TILE] = parts[0]
        out[:, TILE : TILE + 128] = parts[1]

    top, bottom = message(0), message(1)

    @pl.when(row % 2 == 0)
    def _():
        put(even_out, bottom)
        put(odd_out, top)

    @pl.when(row % 2 == 1)
    def _():
        put(even_out, top)
        put(odd_out, bottom)


def centre_kernel(terms, blur, direct, th, tl, images, other, *refs):
    if terms[0]:
        out, yh, yl = refs
        plain = other[...]
    else:
        row_band, col_band, out, yh, yl = refs
        row_band[...] = coarse_band(lax.axis_index("row"), other[1])
        col_band[...] = coarse_band(lax.axis_index("col"), other[1]) * other[0]
        plain = jnp.zeros((TILE, TILE), F32)
    for n, k in enumerate(terms):
        image = images[k]
        plain = plain + direct[k] * image
        xh, xl = split(image)
        tall = dot(th[k], xh) + (dot(th[k], xl) + dot(tl[k], xh))
        high, low = split(tall * blur[k])
        yh[:, TILE * n : TILE * (n + 1)] = high
        yl[:, TILE * n : TILE * (n + 1)] = low
    some = slice(terms[0], terms[-1] + 1)
    high = th[some].reshape(len(terms) * TILE, TILE)
    low = tl[some].reshape(len(terms) * TILE, TILE)
    for at in (0, TILE // 2):
        rows = slice(at, at + TILE // 2)
        out[rows, :] = plain[rows] + (
            dot(yh[rows, :], high) + (dot(yl[rows, :], high) + dot(yh[rows, :], low))
        )


def centre(terms, *operands):
    scratch = pltpu.VMEM((TILE, len(terms) * TILE), BF16)
    bands = [] if terms[0] else shapes((16, 128), (16, 128))
    return pl.pallas_call(
        functools.partial(centre_kernel, terms),
        out_shape=[*bands, *shapes((TILE, TILE))],
        in_specs=[SCALAR] * 2 + [VECTOR] * 3 + [SCALAR if bands else VECTOR],
        out_specs=[VECTOR] * (len(bands) + 1),
        scratch_shapes=[scratch] * 2,
        cost_estimate=pl.CostEstimate(
            flops=12 * len(terms) * TILE**3, bytes_accessed=1 << 20, transcendentals=0
        ),
        compiler_params=pltpu.CompilerParams(vmem_limit_bytes=8 << 20),
        name="blur_centre",
    )(*operands)


def stacked(parts):
    return jnp.concatenate([*parts, jnp.zeros((128 - 16 * len(parts), 128), F32)], axis=0)


def middle_kernel(band, even, odd, far_a, far_b, own, side, even_out, odd_out, far_out):
    row, col = lax.axis_index("row"), lax.axis_index("col")
    parts = stacked([own[...], even[:, TILE:], odd[:, TILE:], far_a[...], far_b[...]])
    cells = dot3(band[...], parts)
    lane = lax.broadcasted_iota(jnp.int32, (16, 128), 1)
    cells = jnp.where(lane < 16, cells, 0.0)
    turned = jnp.transpose(stacked([cells]))[0:16]
    far_out[...] = turned
    is_even = row % 2 == 0
    tail_e, tail_o = even[:, TILE:], odd[:, TILE:]
    above = jnp.where(row > 0, jnp.where(is_even, tail_o, tail_e), 0.0)
    below = jnp.where(row < COUNT - 1, jnp.where(is_even, tail_e, tail_o), 0.0)
    blank = jnp.zeros((16, TILE - 32), F32)

    def strip(n):
        at = 16 * (n + 1)
        more = jnp.concatenate([above[:, at : at + 16], blank, below[:, at : at + 16]], axis=1)
        return side[16 * n : 16 * n + 16] + more

    left, right = strip(0), strip(1)
    even_out[:, TILE:] = turned
    odd_out[:, TILE:] = turned

    @pl.when(col % 2 == 0)
    def _():
        even_out[:, 0:TILE] = right
        odd_out[:, 0:TILE] = left

    @pl.when(col % 2 == 1)
    def _():
        even_out[:, 0:TILE] = left
        odd_out[:, 0:TILE] = right


def last_kernel(band, up, local, row_e, row_o, col_e, col_o, far_a, far_b, own, out):
    row, col = lax.axis_index("row"), lax.axis_index("col")
    parts = stacked([own[...], col_e[:, TILE:], col_o[:, TILE:], far_a[...], far_b[...]])
    cells = dot3(band[...], parts)
    pad = jnp.zeros((112, TILE), F32)
    lines = dot3(cells, jnp.concatenate([up[variant(row)], pad], axis=0))
    is_even = col % 2 == 0
    strip_e, strip_o = col_e[:, 0:TILE], col_o[:, 0:TILE]
    left = jnp.where(col > 0, jnp.where(is_even, strip_o, strip_e), 0.0)
    right = jnp.where(col < COUNT - 1, jnp.where(is_even, strip_e, strip_o), 0.0)
    turned = jnp.transpose(
        jnp.concatenate([left, pad[0:16], lines, pad[0:64], right], axis=0)
    )
    spread = jnp.concatenate([pad[0:32], up[variant(col)], pad[0:80]], axis=0)
    lane = lax.broadcasted_iota(jnp.int32, (TILE, 128), 1)
    whole = local[...] + dot3(jnp.where((lane >= 32) & (lane < 48), turned, 0.0), spread)
    out[:, 0:128] = whole[:, 0:128] + jnp.where(lane < 16, turned, 0.0)
    out[:, 128:TILE] = whole[:, 128:TILE] + jnp.where(lane >= 112, turned, 0.0)
    is_even = row % 2 == 0
    strip_e, strip_o = row_e[:, 0:TILE], row_o[:, 0:TILE]
    out[0:16, :] += jnp.where(row > 0, jnp.where(is_even, strip_o, strip_e), 0.0)
    out[TILE - 16 : TILE, :] += jnp.where(
        row < COUNT - 1, jnp.where(is_even, strip_e, strip_o), 0.0
    )


SCALAR = pl.BlockSpec(memory_space=pltpu.SMEM)
VECTOR = pl.BlockSpec(memory_space=pltpu.VMEM)


def shapes(*dims):
    return [jax.ShapeDtypeStruct(d, F32) for d in dims]


def apart(values):
    return pltpu.with_memory_space_constraint(values, pltpu.HBM)


def swap(values, axis, step, phase):
    return lax.ppermute(values, ("row", "col"), swap_pairs(axis, step, phase))


def on_device(term_images, blur_width, blur_coef, direct_coef, long_weight, long_gain, long_width):
    message, tiny = (16, TILE + 128), (16, 128)
    banded = jax.ShapeDtypeStruct((K, TILE, TILE), BF16)
    even, odd, far, side, th, tl, held = pl.pallas_call(
        first_kernel,
        out_shape=[
            *shapes(message, message, tiny, (32, TILE)),
            banded,
            banded,
            jax.ShapeDtypeStruct((K, TILE, TILE), F32),
        ],
        in_specs=[
            *[pl.BlockSpec(memory_space=pltpu.HBM)] * 5,
        ],
        out_specs=[VECTOR] * 7,
        scratch_shapes=[
            pltpu.VMEM((32, K * TILE), BF16),
            pltpu.VMEM((32, K * TILE), BF16),
            pltpu.VMEM((TILE, 2 * TILE + 128), F32),
            *[pltpu.SMEM((K,), F32)] * 3,
            pltpu.VMEM((2, 16, TILE), F32),
            pltpu.SemaphoreType.DMA((K + 5,)),
        ],
        compiler_params=pltpu.CompilerParams(vmem_limit_bytes=16 << 20),
        name="blur_edges",
    )(
        *[apart(value) for value in (blur_width, blur_coef, long_weight)],
        apart(jnp.asarray(DOWN)),
        apart(term_images),
    )
    row_e, row_o = swap(even, "row", 1, 0), swap(odd, "row", 1, 1)
    row_a, row_b = swap(far, "row", 2, 0), swap(far, "row", 2, 1)
    long_range = jnp.concatenate([long_gain, long_width])
    row_band, col_band, local = centre(
        (0, 1, 2, 3), blur_coef, direct_coef, th, tl, held, long_range
    )
    even, odd, turned = pl.pallas_call(
        middle_kernel,
        out_shape=shapes(message, message, tiny),
        in_specs=[VECTOR] * 7,
        out_specs=[VECTOR] * 3,
        compiler_params=pltpu.CompilerParams(vmem_limit_bytes=4 << 20),
        name="join_rows",
    )(row_band, row_e, row_o, row_a, row_b, far, side)
    col_e, col_o = swap(even, "col", 1, 0), swap(odd, "col", 1, 1)
    col_a, col_b = swap(turned, "col", 2, 0), swap(turned, "col", 2, 1)
    (local,) = centre((4, 5, 6, 7), blur_coef, direct_coef, th, tl, held, local)
    return pl.pallas_call(
        last_kernel,
        out_shape=jax.ShapeDtypeStruct((TILE, TILE), F32),
        in_specs=[VECTOR] * 10,
        out_specs=VECTOR,
        compiler_params=pltpu.CompilerParams(vmem_limit_bytes=8 << 20),
        name="join_columns",
    )(col_band, jnp.asarray(UP), local, row_e, row_o, col_e, col_o, col_a, col_b, turned)


def solution(mesh):
    placed = (P(None, "row", "col"), P(), P(), P(), P(), P(), P())
    return jax.shard_map(
        on_device, mesh=mesh, in_specs=placed, out_specs=P("row", "col"), check_vma=False
    )
```

```python
import functools
import jax
import jax.numpy as jnp
import numpy as np
from jax import lax
from jax.experimental import pallas as pl
from jax.experimental.pallas import tpu as pltpu
from jax.sharding import PartitionSpec as P

K = 8
REACH = 16
LEVELS = 5
RC = 8
TILE = 256
CELLS = TILE >> LEVELS
SPAN = CELLS + 3
COUNT = 16
FIRST, SECOND = (0, 1, 2, 3), (4, 5, 6, 7)
F32 = jnp.float32
BF16 = jnp.bfloat16


def pyramid_matrices():
    size = 4 * TILE
    down = np.eye(size)
    for _ in range(LEVELS):
        count = down.shape[0] // 2
        step = np.zeros((count, 2 * count))
        for i in range(count):
            for t, value in enumerate((1, 4, 6, 4, 1)):
                if 0 <= 2 * i + t - 2 < 2 * count:
                    step[i, 2 * i + t - 2] = value / 16
        down = step @ down
    up = np.eye(size >> LEVELS)
    for _ in range(LEVELS):
        count = up.shape[0]
        step = np.zeros((2 * count, count))
        for i in range(count):
            for j, value in ((i - 1, 1 / 8), (i, 6 / 8), (i + 1, 1 / 8)):
                if 0 <= j < count:
                    step[2 * i, j] = value
            for j in (i, i + 1):
                if j < count:
                    step[2 * i + 1, j] = 1 / 2
        up = step @ up
    down_tiles, up_tiles = np.zeros((3, 16, TILE)), np.zeros((3, 16, TILE))
    for n, tile in enumerate((0, 1, 3)):
        pixels = slice(tile * TILE, (tile + 1) * TILE)
        for i in range(SPAN):
            line = tile * CELLS - 1 + i
            if 0 <= line < size >> LEVELS:
                down_tiles[n, i] = down[line, pixels]
                up_tiles[n, i] = up[pixels, line]
        assert np.isclose(down_tiles[n].sum(), down[:, pixels].sum())
        assert np.isclose(up_tiles[n].sum(), up[pixels].sum())
    return down_tiles.astype(np.float32), up_tiles.astype(np.float32)


DOWN, UP = pyramid_matrices()
TALL = np.pad(UP.transpose(0, 2, 1), ((0, 0), (0, 0), (0, 112)))


def swap_pairs(axis, step, phase):
    partner = {}
    for i in range(COUNT - step):
        if (i // step) % 2 == phase:
            partner[i], partner[i + step] = i + step, i
    pairs = []
    for r in range(COUNT):
        for c in range(COUNT):
            if (r if axis == "row" else c) in partner:
                other = (partner[r], c) if axis == "row" else (r, partner[c])
            else:
                other = (r, c ^ 1) if axis == "row" and step == 1 else (r ^ 1, c)
            pairs.append((r * COUNT + c, other[0] * COUNT + other[1]))
    return pairs


def deltas(at):
    one = jnp.where(at % 2 == 0, 1, -1)
    two = jnp.where((at // 2) % 2 == 0, 2, -2)
    return (0, one, -one, two, -two)


def split(values):
    high = values.astype(BF16)
    return high, (values - high.astype(F32)).astype(BF16)


def dot(a, b, transposed=False):
    dims = (((1,), (1 if transposed else 0,)), ((), ()))
    return lax.dot_general(a, b, dims, preferred_element_type=F32)


def dot3(a, b, transposed=False):
    (ah, al), (bh, bl) = split(a), split(b)
    return dot(ah, bh, transposed) + (dot(ah, bl, transposed) + dot(al, bh, transposed))


def variant(at):
    return jnp.where(at == 0, 0, jnp.where(at == COUNT - 1, 2, 1))


def gauss(offsets, width, reach):
    wide = jnp.full((1, 128), width, F32)
    scale = -0.5 / (wide * wide)
    taps = (lax.broadcasted_iota(jnp.int32, (1, 128), 1) - reach).astype(F32)
    total = jnp.sum(
        jnp.where(jnp.abs(taps) <= reach, jnp.exp(taps * taps * scale), 0.0), axis=1, keepdims=True
    )
    far = offsets.astype(F32)
    values = jnp.exp(far * far * scale) * (1.0 / total)
    return jnp.where(jnp.abs(far) <= reach, values, 0.0)


def coarse_band(at, width):
    line = lax.broadcasted_iota(jnp.int32, (16, 128), 0)
    lane = lax.broadcasted_iota(jnp.int32, (16, 128), 1)
    block, cell = lane // 16, lane % 16
    delta = jnp.zeros((16, 128), jnp.int32)
    for n, value in enumerate(deltas(at)):
        delta = jnp.where(block == n, value, delta)
    inside = (at + delta >= 0) & (at + delta < COUNT) & (block < 5) & (cell < SPAN) & (line < SPAN)
    return jnp.where(inside, gauss(8 * delta + cell - line, width * RC, RC), 0.0)


def edge_band(width):
    line = lax.broadcasted_iota(jnp.int32, (32, TILE), 0)
    lane = lax.broadcasted_iota(jnp.int32, (32, TILE), 1)
    image, place = lane // 32, lane % 32
    wide = jnp.full((32, TILE), width[0], F32)
    for k in range(1, K):
        wide = jnp.where(image == k, width[k], wide)
    scale = -0.5 / (wide * wide)
    far = jnp.where(line < 16, place + 16 - line, place - 16 - line)
    valid = (jnp.abs(far) <= REACH) & ((line < 16) == (place < 16))
    row_scale = scale[0:8]
    total = jnp.full((8, TILE), 0.5, F32)
    for t in range(1, REACH + 1):
        total = total + jnp.exp(float(t * t) * row_scale)
    share = 0.5 / total
    share = jnp.concatenate([share] * 4, axis=0)
    far = far.astype(F32)
    return jnp.where(valid, jnp.exp(far * far * scale) * share, 0.0)


def first_kernel(
    width_in, blur_in, weight_in, down_in, images,
    even_out, odd_out, far_out, side_out, th, tl, held,
    eh, el, zone, width, blur, weight, down, sems,
):
    row, col = lax.axis_index("row"), lax.axis_index("col")
    small = [
        pltpu.make_async_copy(source, target, sems.at[K + n])
        for n, (source, target) in enumerate(
            (
                (width_in, width),
                (blur_in, blur),
                (weight_in, weight),
                (down_in.at[variant(row)], down.at[0]),
                (down_in.at[variant(col)], down.at[1]),
            )
        )
    ]
    copies = [pltpu.make_async_copy(images.at[k], held.at[k], sems.at[k]) for k in range(K)]
    for copy in small + copies:
        copy.start()
    for copy in small:
        copy.wait()
    half = TILE // 2
    offsets = (
        lax.broadcasted_iota(jnp.int32, (half + 32, 128), 1)
        - lax.broadcasted_iota(jnp.int32, (half + 32, 128), 0)
        + REACH
    )
    none = jnp.zeros((half, 128), BF16)
    for k in range(K):
        for full, edge, band in zip((th, tl), (eh, el), split(gauss(offsets, width[k], REACH))):
            full[k, 0 : half + 16, 0:half] = band[16 : half + 32]
            full[k, half + 16 : TILE, 0:half] = none[16:]
            full[k, 0 : half - 16, half:TILE] = none[16:]
            full[k, half - 16 : TILE, half:TILE] = band[0 : half + 16]
            edge[0:16, TILE * k : TILE * k + half] = band[0:16]
            edge[0:16, TILE * k + half : TILE * (k + 1)] = none[0:16]
            edge[16:32, TILE * k : TILE * k + half] = none[0:16]
            edge[16:32, TILE * k + half : TILE * (k + 1)] = band[half + 16 : half + 32]
    ends = split(edge_band(width))
    zone[:, 2 * TILE :] = jnp.zeros((TILE, 128), F32)
    lane = lax.broadcasted_iota(jnp.int32, (TILE, 128), 1)
    source = jnp.zeros((TILE, TILE), F32)
    for k in range(K):
        if k % 4 == 0:
            for copy in copies[k : k + 4]:
                copy.wait()
        image = held[k]
        source = source + weight[k] * image * image
        turned = jnp.transpose(jnp.where(lane < 64, image[:, 0:128], image[:, 128:TILE]))
        lines = [image[0:16], image[TILE - 16 : TILE], turned[0:16], turned[112:128]]
        ah, al = split(jnp.concatenate(lines, axis=0) * blur[k])
        done = dot(ah, th[k]) + (dot(al, th[k]) + dot(ah, tl[k]))
        zone[32 * k : 32 * k + 32, 0:TILE] = done[0:32]
        zone[32 * k : 32 * k + 32, TILE : 2 * TILE] = done[32:64]
        part = slice(TILE * k, TILE * (k + 1))
        zone[32 * k : 32 * k + 32, 2 * TILE : 2 * TILE + 32] = dot(
            ah[32:64], eh[:, part], True
        ) + (dot(al[32:64], eh[:, part], True) + dot(ah[32:64], el[:, part], True))
    zh, zl = split(zone[...])
    strips = dot(ends[0], zh) + (dot(ends[1], zh) + dot(ends[0], zl))
    side_out[...] = strips[:, TILE : 2 * TILE]
    cells = dot3(dot3(down[0], source), down[1], True)
    far_out[...] = jnp.concatenate([cells, jnp.zeros((16, 112), F32)], axis=1)

    def message(n):
        at = 2 * TILE + 16 * n
        corners = [strips[0:16, at : at + 16], strips[16:32, at : at + 16]]
        tail = jnp.concatenate([cells, *corners, jnp.zeros((16, 80), F32)], axis=1)
        return strips[16 * n : 16 * n + 16, 0:TILE], tail

    def put(out, parts):
        out[:, 0:TILE] = parts[0]
        out[:, TILE : TILE + 128] = parts[1]

    top, bottom = message(0), message(1)

    @pl.when(row % 2 == 0)
    def _():
        put(even_out, bottom)
        put(odd_out, top)

    @pl.when(row % 2 == 1)
    def _():
        put(even_out, top)
        put(odd_out, bottom)


def centre_kernel(terms, blur, direct, other, th, tl, images, *refs):
    if terms[0]:
        base, up, band_in, spread, out, yh, yl = refs
        plain = base[...]
        band = jnp.transpose(stacked([band_in[...] * other[0]]))
        across = up[variant(lax.axis_index("col"))]
        across = jnp.concatenate([across, jnp.zeros((112, TILE), F32)], axis=0)
        spread[...] = dot3(band, across)
    else:
        row_band, col_band, out, yh, yl = refs
        row_band[...] = coarse_band(lax.axis_index("row"), other[0])
        col_band[...] = coarse_band(lax.axis_index("col"), other[0])
        plain = jnp.zeros((TILE, TILE), F32)
    for n, k in enumerate(terms):
        image = images[k]
        plain = plain + direct[k] * image
        xh, xl = split(image)
        tall = dot(th[k], xh) + (dot(th[k], xl) + dot(tl[k], xh))
        high, low = split(tall * blur[k])
        yh[:, TILE * n : TILE * (n + 1)] = high
        yl[:, TILE * n : TILE * (n + 1)] = low
    some = slice(terms[0], terms[-1] + 1)
    high = th[some].reshape(len(terms) * TILE, TILE)
    low = tl[some].reshape(len(terms) * TILE, TILE)
    for at in (0, TILE // 2):
        rows = slice(at, at + TILE // 2)
        out[rows, :] = plain[rows] + (
            dot(yh[rows, :], high) + (dot(yl[rows, :], high) + dot(yh[rows, :], low))
        )


def centre(terms, *operands):
    scratch = pltpu.VMEM((TILE, len(terms) * TILE), BF16)
    bands = shapes((128, TILE)) if terms[0] else shapes((16, 128), (16, 128))
    return pl.pallas_call(
        functools.partial(centre_kernel, terms),
        out_shape=[*bands, *shapes((TILE, TILE))],
        in_specs=[SCALAR] * 3 + [VECTOR] * (len(operands) - 3),
        out_specs=[VECTOR] * (len(bands) + 1),
        scratch_shapes=[scratch] * 2,
        cost_estimate=pl.CostEstimate(
            flops=12 * len(terms) * TILE**3, bytes_accessed=1 << 20, transcendentals=0
        ),
        compiler_params=pltpu.CompilerParams(vmem_limit_bytes=8 << 20),
        name="blur_centre",
    )(*operands)


def stacked(parts):
    return jnp.concatenate([*parts, jnp.zeros((128 - 16 * len(parts), 128), F32)], axis=0)


def middle_kernel(band, even, odd, far_a, far_b, own, side, even_out, odd_out, far_out):
    row, col = lax.axis_index("row"), lax.axis_index("col")
    parts = stacked([own[...], even[:, TILE:], odd[:, TILE:], far_a[...], far_b[...]])
    cells = dot3(band[...], parts)
    lane = lax.broadcasted_iota(jnp.int32, (16, 128), 1)
    cells = jnp.where(lane < 16, cells, 0.0)
    far_out[...] = cells
    is_even = row % 2 == 0
    tail_e, tail_o = even[:, TILE:], odd[:, TILE:]
    above = jnp.where(row > 0, jnp.where(is_even, tail_o, tail_e), 0.0)
    below = jnp.where(row < COUNT - 1, jnp.where(is_even, tail_e, tail_o), 0.0)
    blank = jnp.zeros((16, TILE - 32), F32)

    def strip(n):
        at = 16 * (n + 1)
        more = jnp.concatenate([above[:, at : at + 16], blank, below[:, at : at + 16]], axis=1)
        return side[16 * n : 16 * n + 16] + more

    left, right = strip(0), strip(1)
    even_out[:, TILE:] = cells
    odd_out[:, TILE:] = cells

    @pl.when(col % 2 == 0)
    def _():
        even_out[:, 0:TILE] = right
        odd_out[:, 0:TILE] = left

    @pl.when(col % 2 == 1)
    def _():
        even_out[:, 0:TILE] = left
        odd_out[:, 0:TILE] = right


def last_kernel(spread, up, local, row_e, row_o, col_e, col_o, far_a, far_b, own, out):
    row, col = lax.axis_index("row"), lax.axis_index("col")
    cells = own[...]
    for n, part in enumerate((col_e[:, TILE:], col_o[:, TILE:], far_a[...], far_b[...])):
        cells = cells + pltpu.roll(part, 16 * (n + 1), 1)
    lines = dot3(cells, spread[...])
    lines = jnp.concatenate([lines, jnp.zeros((112, TILE), F32)], axis=0)
    whole = local[...] + dot3(up[variant(row)], lines)
    is_even = col % 2 == 0
    strip_e, strip_o = col_e[:, 0:TILE], col_o[:, 0:TILE]
    left = jnp.where(col > 0, jnp.where(is_even, strip_o, strip_e), 0.0)
    right = jnp.where(col < COUNT - 1, jnp.where(is_even, strip_e, strip_o), 0.0)
    turned = jnp.transpose(
        jnp.concatenate([left, jnp.zeros((96, TILE), F32), right], axis=0)
    )
    lane = lax.broadcasted_iota(jnp.int32, (TILE, 128), 1)
    out[:, 0:128] = whole[:, 0:128] + jnp.where(lane < 16, turned, 0.0)
    out[:, 128:TILE] = whole[:, 128:TILE] + jnp.where(lane >= 112, turned, 0.0)
    is_even = row % 2 == 0
    strip_e, strip_o = row_e[:, 0:TILE], row_o[:, 0:TILE]
    out[0:16, :] += jnp.where(row > 0, jnp.where(is_even, strip_o, strip_e), 0.0)
    out[TILE - 16 : TILE, :] += jnp.where(
        row < COUNT - 1, jnp.where(is_even, strip_e, strip_o), 0.0
    )


SCALAR = pl.BlockSpec(memory_space=pltpu.SMEM)
VECTOR = pl.BlockSpec(memory_space=pltpu.VMEM)


def shapes(*dims):
    return [jax.ShapeDtypeStruct(d, F32) for d in dims]


def apart(values):
    return pltpu.with_memory_space_constraint(values, pltpu.HBM)


def swap(values, axis, step, phase):
    return lax.ppermute(values, ("row", "col"), swap_pairs(axis, step, phase))


def on_device(term_images, blur_width, blur_coef, direct_coef, long_weight, long_gain, long_width):
    message, tiny = (16, TILE + 128), (16, 128)
    banded = jax.ShapeDtypeStruct((K, TILE, TILE), BF16)
    even, odd, far, side, th, tl, held = pl.pallas_call(
        first_kernel,
        out_shape=[
            *shapes(message, message, tiny, (32, TILE)),
            banded,
            banded,
            jax.ShapeDtypeStruct((K, TILE, TILE), F32),
        ],
        in_specs=[
            *[pl.BlockSpec(memory_space=pltpu.HBM)] * 5,
        ],
        out_specs=[VECTOR] * 7,
        scratch_shapes=[
            pltpu.VMEM((32, K * TILE), BF16),
            pltpu.VMEM((32, K * TILE), BF16),
            pltpu.VMEM((TILE, 2 * TILE + 128), F32),
            *[pltpu.SMEM((K,), F32)] * 3,
            pltpu.VMEM((2, 16, TILE), F32),
            pltpu.SemaphoreType.DMA((K + 5,)),
        ],
        compiler_params=pltpu.CompilerParams(vmem_limit_bytes=16 << 20),
        name="blur_edges",
    )(
        *[apart(value) for value in (blur_width, blur_coef, long_weight)],
        apart(jnp.asarray(DOWN)),
        apart(term_images),
    )
    row_e, row_o = swap(even, "row", 1, 0), swap(odd, "row", 1, 1)
    row_a, row_b = swap(far, "row", 2, 0), swap(far, "row", 2, 1)
    row_band, col_band, local = centre(
        FIRST, blur_coef, direct_coef, long_width, th, tl, held
    )
    even, odd, turned = pl.pallas_call(
        middle_kernel,
        out_shape=shapes(message, message, tiny),
        in_specs=[VECTOR] * 7,
        out_specs=[VECTOR] * 3,
        compiler_params=pltpu.CompilerParams(vmem_limit_bytes=4 << 20),
        name="join_rows",
    )(row_band, row_e, row_o, row_a, row_b, far, side)
    col_e, col_o = swap(even, "col", 1, 0), swap(odd, "col", 1, 1)
    col_a, col_b = swap(turned, "col", 2, 0), swap(turned, "col", 2, 1)
    spread, local = centre(
        SECOND, blur_coef, direct_coef, long_gain, th, tl, held, local, jnp.asarray(UP), col_band
    )
    return pl.pallas_call(
        last_kernel,
        out_shape=jax.ShapeDtypeStruct((TILE, TILE), F32),
        in_specs=[VECTOR] * 10,
        out_specs=VECTOR,
        compiler_params=pltpu.CompilerParams(vmem_limit_bytes=8 << 20),
        name="join_columns",
    )(spread, jnp.asarray(TALL), local, row_e, row_o, col_e, col_o, col_a, col_b, turned)


def solution(mesh):
    placed = (P(None, "row", "col"), P(), P(), P(), P(), P(), P())

    return jax.shard_map(
        on_device, mesh=mesh, in_specs=placed, out_specs=P("row", "col"), check_vma=False
    )
```
